512 devices in a mesh: blk: 64 (over y_hi, z, core), fld: 8 (over x, y_lo).
Axes of the slice: x: 4, y: 4 (y_hi: 2, y_lo: 2; y = y_hi * 2 + y_lo), z: 16, core: 2. Of those that a mesh axis runs over, the one named last changes fastest.
Arguments:
- vectors: bfloat16 [4096, 16384], P('blk', 'fld'), may hold values from -1.1953125 to 1.1953125
- norms: bfloat16 [4096], P('blk'), may hold values from 0.5 to 2
- offsets: int32 [2], replicated, may hold values from 1 to 31
- pivot_block: int32 [2, 3], replicated, may hold values from 0 to 63
- pivot_row: int32 [2, 3], replicated, may hold values from 0 to 63
Outputs:
- similarity: bfloat16 [2, 3, 4096, 64], P(None, None, ('blk', 'fld'))
The draws below stay inside these ranges and needn't reach their ends.
All inputs are finite; a program needn't handle non-finite values.
Results may differ from the reference program's by a relative error of at most 0.014.
Values may be sent and summed in bfloat16 or wider, within the bound.
No kernel may reach another device: no remote copies, remote signals or barrier semaphores. Data moves between devices by JAX's collectives and lax.ppermute only.
A program may use at most 64 MiB of HBM per device.

```python
import math
import jax
import jax.numpy as jnp
from jax import lax

F = 16384
VB = 64
PIV = 3
NOFF = 2
NV = 4096
N_BLK = 64
N_FLD = 8


def place_ends(entries, rng, least, high):
    shape = entries.shape
    spot = [jax.random.randint(jax.random.fold_in(rng, axis), (), 0, shape[axis]) for axis in range(len(shape))]
    entries = entries.at[tuple(spot)].set(least)
    longest = shape.index(max(shape))
    spot[longest] = (spot[longest] + 1) % shape[longest]
    return entries.at[tuple(spot)].set(high)


def block_scale(own_key, extent, cuts, low, high):
    loudness, own = 1.0, jax.random.fold_in(own_key, 6)
    for dim, parts in cuts:
        draws = jnp.exp(jax.random.uniform(jax.random.fold_in(own, dim), (parts,), jnp.float32, low / len(cuts), high / len(cuts)))
        loudness = loudness * jnp.repeat(draws, extent[dim] // parts).reshape([-1 if axis == dim else 1 for axis in range(len(extent))])
    return loudness


def gaussian(own_key, dims, deviation, reach, shards=(), held_as=jnp.bfloat16):
    entries = jax.random.normal(own_key, dims, jnp.float32) * deviation
    if len(shards) > 0:
        entries = block_scale(own_key, dims, shards, -0.22, 0.18) * entries
    return jnp.clip(entries, min=-reach, max=reach).astype(held_as)


def setup_inputs(seed: int = 0) -> dict:
    key_of = jax.random.split(jax.random.key(seed), 6)
    vectors = gaussian(key_of[0], (NV, F), 0.2, 1.1953125, ((0, 64), (1, 8)))
    norms = jnp.clip(jnp.exp(math.log(2.0) - 1.3862944 * jax.random.uniform(key_of[1], (NV,), jnp.float32) ** block_scale(key_of[1], (NV,), ((0, 64),), -0.2, 0.2)), 0.5, 2.0).astype(jnp.bfloat16)
    offsets = jax.random.randint(key_of[2], (NOFF,), 1, N_BLK // 2).astype(jnp.int32)
    pivot_block = place_ends(jax.random.randint(key_of[3], (NOFF, PIV), 0, N_BLK), jax.random.fold_in(key_of[3], 1), 0, N_BLK - 1).astype(jnp.int32)
    pivot_row = place_ends(jax.random.randint(key_of[4], (NOFF, PIV), 0, VB), jax.random.fold_in(key_of[4], 1), 0, VB - 1).astype(jnp.int32)
    return dict(vectors=vectors, norms=norms, offsets=offsets, pivot_block=pivot_block, pivot_row=pivot_row)


def reference(vectors, norms, offsets, pivot_block, pivot_row):
    fd = F // N_FLD
    flat_index = (pivot_block * VB + pivot_row).reshape(-1).astype(jnp.int32)
    pivots = vectors[flat_index].astype(jnp.float32).reshape(NOFF, PIV, F)
    pivot_norms = norms[flat_index].astype(jnp.float32).reshape(NOFF, PIV)

    def one_block(block):
        start = (block * VB).astype(jnp.int32)
        resident = lax.dynamic_slice_in_dim(vectors, start, VB, 0)
        resident_norms = lax.dynamic_slice_in_dim(norms, start, VB, 0).astype(jnp.float32)

        def partner_of(offset):
            first = (((block + offset) % N_BLK) * VB).astype(jnp.int32)
            return (lax.dynamic_slice_in_dim(vectors, first, VB, 0),
                    lax.dynamic_slice_in_dim(norms, first, VB, 0))

        partners, partner_norms = jax.vmap(partner_of)(offsets)
        scaled = (resident.astype(jnp.float32)[None, None] * pivots[:, :, None, :]).astype(jnp.bfloat16)
        scaled = scaled.astype(jnp.float32).reshape(NOFF, PIV, VB, N_FLD, fd)
        partner_f = partners.astype(jnp.float32).reshape(NOFF, VB, N_FLD, fd)
        sums = jnp.einsum("tsinq,tknq->tsnik", scaled, partner_f, precision=lax.Precision.HIGHEST)
        rounded = lax.optimization_barrier(sums.astype(jnp.bfloat16))
        field_sum = jnp.sum(rounded.astype(jnp.float32), axis=2)
        denominator = (resident_norms[None, None, :, None] * pivot_norms[:, :, None, None]) * partner_norms.astype(jnp.float32)[:, None, None, :]
        return (field_sum / denominator).astype(jnp.bfloat16)

    tiles = lax.map(one_block, jnp.arange(N_BLK, dtype=jnp.int32))
    return jnp.transpose(tiles, (1, 2, 0, 3, 4)).reshape(NOFF, PIV, NV, VB)
```

```python
import functools

import jax
import jax.numpy as jnp
from jax import lax
from jax.sharding import PartitionSpec as P

NOFF = 2


def blk_groups(kind):
    at = lambda y, z, c: (y * 16 + z) * 2 + c
    if kind == "near":
        return [[at(y, z, c) for y in range(2) for c in range(2)] for z in range(16)]
    return [[at(y, z, c) for z in range(16)] for y in range(2) for c in range(2)]


def spread(rows):
    near, along = blk_groups("near"), blk_groups("z")
    n, m = len(near[0]), len(along[0])
    count, fields = rows.shape
    parts = rows.reshape(count, n, fields // n).transpose(1, 0, 2)
    got = lax.all_to_all(parts, "blk", 0, 0, axis_index_groups=near)
    share = got.astype(jnp.float32).sum(0).astype(jnp.bfloat16)
    got = lax.all_to_all(
        jnp.broadcast_to(share[None], (m,) + share.shape), "blk", 0, 0, axis_index_groups=along
    )
    share = got.astype(jnp.float32).sum(0).astype(jnp.bfloat16)
    got = lax.all_to_all(
        jnp.broadcast_to(share[None], (n,) + share.shape), "blk", 0, 0, axis_index_groups=near
    )
    return got.transpose(1, 0, 2).reshape(count, fields)


def shifted(value, by):
    peers = lax.axis_size("blk")
    if by % peers == 0:
        return value
    return lax.ppermute(value, "blk", [(i, (i - by) % peers) for i in range(peers)])


def body(vectors, norms, offsets, pivot_block, pivot_row):
    rows, fields = vectors.shape
    blocks = lax.axis_size("blk")
    slices = lax.axis_size("fld")
    place = lax.axis_index("fld")
    block = lax.axis_index("blk")
    share = rows // slices
    count_piv = pivot_block.shape[1]
    steps = NOFF * count_piv
    flat_block = pivot_block.reshape(-1)
    flat_row = pivot_row.reshape(-1)

    picks = [lax.dynamic_slice(vectors, (flat_row[s], 0), (1, fields)) for s in range(steps)]
    own = jnp.concatenate(picks, 0)
    own = jnp.where((flat_block == block)[:, None], own, jnp.zeros_like(own))
    table = lax.dynamic_update_slice(
        jnp.zeros((blocks * rows,), jnp.bfloat16), norms, (block * rows,)
    ).reshape(-1, fields)
    every = spread(jnp.concatenate([own, table], 0))
    pivots = every[:steps]
    all_norms = every[steps:].reshape(-1).astype(jnp.float32)

    far = blocks // 2
    pull = [functools.partial(shifted, by=k) for k in range(1, far)]
    partners = [lax.switch(offsets[t] - 1, pull, vectors) for t in range(NOFF)]

    out = []
    for t in range(NOFF):
        mine = pivots[t * count_piv : (t + 1) * count_piv].astype(jnp.float32)
        scaled = (vectors.astype(jnp.float32)[None] * mine[:, None, :]).astype(jnp.bfloat16)
        out.append(
            lax.dot_general(
                scaled.reshape(count_piv * rows, fields),
                partners[t],
                (((1,), (1,)), ((), ())),
                preferred_element_type=jnp.float32,
            ).astype(jnp.bfloat16)
        )
    sums = jnp.stack(out).reshape(steps, slices, share, rows).transpose(1, 0, 2, 3)
    got = lax.all_to_all(sums, "fld", 0, 0)
    field_sum = got.astype(jnp.float32).sum(0)

    own_norms = lax.dynamic_slice_in_dim(norms, place * share, share, 0).astype(jnp.float32)
    pivot_norms = jnp.stack(
        [lax.dynamic_index_in_dim(all_norms, flat_block[s] * rows + flat_row[s], 0, False) for s in range(steps)]
    )
    partner_norms = jnp.stack(
        [lax.dynamic_slice_in_dim(all_norms, (block + offsets[t]) % blocks * rows, rows, 0) for t in range(NOFF)]
    )
    partner_norms = jnp.repeat(partner_norms, count_piv, axis=0)
    denominator = (own_norms[None, :, None] * pivot_norms[:, None, None]) * partner_norms[:, None, :]
    result = (field_sum / denominator).astype(jnp.bfloat16)
    return result.reshape(NOFF, count_piv, share, rows)


def solution(mesh):
    return jax.shard_map(
        body,
        mesh=mesh,
        in_specs=(P("blk", "fld"), P("blk"), P(), P(), P()),
        out_specs=P(None, None, ("blk", "fld"), None),
        check_vma=False,
    )
```

```python
import functools

import jax
import jax.numpy as jnp
from jax import lax
from jax.experimental import pallas as pl
from jax.experimental.pallas import tpu as pltpu
from jax.sharding import PartitionSpec as P

NOFF = 2
VMEM = pl.BlockSpec(memory_space=pltpu.VMEM)
SMEM = pl.BlockSpec(memory_space=pltpu.SMEM)


def blk_groups(kind):
    at = lambda y, z, c: (y * 16 + z) * 2 + c
    if kind == "near":
        return [[at(y, z, c) for y in range(2) for c in range(2)] for z in range(16)]
    return [[at(y, z, c) for z in range(16)] for y in range(2) for c in range(2)]


def iota(shape, dim):
    return lax.broadcasted_iota(jnp.int32, shape, dim)


def prepare_kernel(block_ref, row_ref, v_ref, norms_ref, out_ref):
    block = lax.axis_index("blk")
    rows, fields = v_ref.shape
    per_row = fields // rows
    lines, steps = 8, 6
    line, lane = iota((lines, rows), 0), iota((lines, rows), 1)
    pick = jnp.zeros((lines, rows), jnp.float32)
    for s in range(steps):
        mine = block_ref[s // 3, s % 3] == block
        wanted = jnp.where(mine, row_ref[s // 3, s % 3], -1)
        pick = jnp.where((line == s) & (lane == wanted), 1.0, pick)
    held = jnp.broadcast_to(norms_ref[...].astype(jnp.float32), (lines, rows))
    held = jnp.where(line == steps + block // per_row, held, 0.0)
    place = iota((rows, fields), 1) - block % per_row * rows
    spots = jnp.where(place == iota((rows, fields), 0), 1.0, 0.0).astype(jnp.bfloat16)
    total = jnp.dot(pick.astype(jnp.bfloat16), v_ref[...], preferred_element_type=jnp.float32)
    total += jnp.dot(held.astype(jnp.bfloat16), spots, preferred_element_type=jnp.float32)
    parts, _, width = out_ref.shape
    for n in range(parts):
        out_ref[n] = total[:, n * width : (n + 1) * width].astype(jnp.bfloat16)


def tiles_kernel(swap_ref, v_ref, first_ref, second_ref, every_ref, out_ref):
    slices, lines, cols = out_ref.shape
    cols = cols // NOFF
    rows, fields = v_ref.shape
    swap = swap_ref[0] == 1
    every = jnp.concatenate([every_ref[n] for n in range(every_ref.shape[0])], axis=1)
    vectors = v_ref[...].astype(jnp.float32)
    found = []
    for partner_ref, t in ((first_ref, 0), (second_ref, 1)):
        scaled = []
        for s in range(3):
            one, other = every[3 * t + s], every[3 * (1 - t) + s]
            pivot = jnp.where(swap, other.astype(jnp.float32), one.astype(jnp.float32))
            scaled.append((vectors * pivot[None, :]).astype(jnp.bfloat16))
        sums = lax.dot_general(
            jnp.concatenate(scaled, 0),
            partner_ref[...],
            (((1,), (1,)), ((), ())),
            preferred_element_type=jnp.float32,
        )
        found.append(sums.reshape(3, slices, rows // slices, cols))
    ordered = jnp.concatenate(
        [jnp.where(swap, found[1], found[0]), jnp.where(swap, found[0], found[1])], 3
    )
    ordered = jnp.transpose(ordered, (1, 0, 2, 3))
    out_ref[...] = ordered.reshape(slices, lines, NOFF * cols).astype(jnp.bfloat16)


def finish_kernel(offset_ref, block_ref, row_ref, got_ref, norms_ref, table_ref, out_ref):
    block, place = lax.axis_index("blk"), lax.axis_index("fld")
    slices, lines, cols = got_ref.shape
    cols = cols // NOFF
    share = cols // slices
    total = got_ref[0].astype(jnp.float32)
    for n in range(1, slices):
        total += got_ref[n].astype(jnp.float32)
    table = table_ref[...].astype(jnp.float32)
    row, lane = iota(table.shape, 0), iota(table.shape, 1)
    entry = row * table.shape[1] + lane
    held = jnp.broadcast_to(norms_ref[...].astype(jnp.float32), (share, cols))
    at = iota((share, cols), 1) == iota((share, cols), 0) + place * share
    own = jnp.sum(jnp.where(at, held, 0.0), axis=1, keepdims=True)
    blocks = table.size // cols
    for t in range(NOFF):
        partner = (block + offset_ref[t]) % blocks
        both = jnp.sum(jnp.where(row == partner // 2, table, 0.0), axis=0, keepdims=True)
        partner_norms = jnp.where(partner % 2 == 1, both[:, cols:], both[:, :cols])
        for s in range(3):
            wanted = block_ref[t, s] * cols + row_ref[t, s]
            pivot = jnp.where(entry == wanted, table, 0.0)
            pivot_norm = jnp.sum(jnp.sum(pivot, axis=0, keepdims=True), axis=1, keepdims=True)
            tile = total[s * share : (s + 1) * share, t * cols : (t + 1) * cols]
            out_ref[t, s] = (tile / ((own * pivot_norm) * partner_norms)).astype(jnp.bfloat16)


def exchange(parts, kind):
    return lax.all_to_all(parts, "blk", 0, 0, axis_index_groups=blk_groups(kind))


def total_of(got, copies):
    total = got.astype(jnp.float32).sum(0).astype(jnp.bfloat16)
    return jnp.broadcast_to(total[None], (copies,) + total.shape)


def shifted(value, by):
    peers = lax.axis_size("blk")
    if by == 0:
        return value
    return lax.ppermute(value, "blk", [(i, (i - by) % peers) for i in range(peers)])


def body(vectors, norms, offsets, pivot_block, pivot_row):
    rows, fields = vectors.shape
    blocks = lax.axis_size("blk")
    slices = lax.axis_size("fld")
    share = rows // slices
    count_piv = pivot_block.shape[1]
    steps = NOFF * count_piv
    near, along = len(blk_groups("near")[0]), len(blk_groups("z")[0])
    half = blocks // 2
    norms_row = norms.reshape(1, rows)

    one, two = offsets[0], offsets[1]
    ring = lambda k: jnp.minimum(k % half, half - k % half)
    direct = ring(one) + ring(two)
    gap = ring(jnp.abs(one - two))
    chained = gap + jnp.minimum(ring(one), ring(two)) < direct
    swap = chained & (ring(two) < ring(one))
    lead = jnp.where(swap, two, one)
    rest = jnp.where(swap, one, two) - jnp.where(chained, lead, 0)

    parts = pl.pallas_call(
        prepare_kernel,
        out_shape=jax.ShapeDtypeStruct((near, 8, fields // near), jnp.bfloat16),
        in_specs=[SMEM, SMEM, VMEM, VMEM],
        out_specs=VMEM,
    )(pivot_block, pivot_row, vectors, norms_row)
    got = exchange(parts, "near")
    got = exchange(total_of(got, along), "z")

    pull = [functools.partial(shifted, by=k) for k in range(1, half)]
    first = lax.switch(lead - 1, pull, vectors)
    got, first = lax.optimization_barrier((got, first))
    got = exchange(total_of(got, near), "near")

    pull = [functools.partial(shifted, by=k) for k in range(2 - half, half)]
    second = lax.switch(rest + half - 2, pull, jnp.where(chained, first, vectors))

    sums = pl.pallas_call(
        tiles_kernel,
        out_shape=jax.ShapeDtypeStruct((slices, count_piv * share, NOFF * rows), jnp.bfloat16),
        in_specs=[SMEM, VMEM, VMEM, VMEM, VMEM],
        out_specs=VMEM,
    )(swap.astype(jnp.int32).reshape(1), vectors, first, second, got)
    table = got[:, steps:].transpose(1, 0, 2).reshape(blocks // 2, 2 * rows)
    got = lax.all_to_all(sums, "fld", 0, 0)

    return pl.pallas_call(
        finish_kernel,
        out_shape=jax.ShapeDtypeStruct((NOFF, count_piv, share, rows), jnp.bfloat16),
        in_specs=[SMEM, SMEM, SMEM, VMEM, VMEM, VMEM],
        out_specs=VMEM,
    )(offsets, pivot_block, pivot_row, got, norms_row, table)


def solution(mesh):
    return jax.shard_map(
        body,
        mesh=mesh,
        in_specs=(P("blk", "fld"), P("blk"), P(), P(), P()),
        out_specs=P(None, None, ("blk", "fld"), None),
        check_vma=False,
    )
```

```python
import jax
import jax.numpy as jnp
from jax import lax
from jax.experimental import pallas as pl
from jax.experimental.pallas import tpu as pltpu
from jax.sharding import PartitionSpec as P

NOFF = 2
VMEM = pl.BlockSpec(memory_space=pltpu.VMEM)
SMEM = pl.BlockSpec(memory_space=pltpu.SMEM)
SMALL = pltpu.CompilerParams(vmem_limit_bytes=16 * 2**20)


def blk_groups(kind):
    at = lambda y, z, c: (y * 16 + z) * 2 + c
    if kind == "near":
        return [[at(y, z, c) for y in range(2) for c in range(2)] for z in range(16)]
    return [[at(y, z, c) for z in range(16)] for y in range(2) for c in range(2)]


def iota(shape, dim):
    return lax.broadcasted_iota(jnp.int32, shape, dim)


def ring(k, half):
    return jnp.minimum(k % half, half - k % half)


def prepare_kernel(offset_ref, block_ref, row_ref, v_ref, norms_ref, plan_ref, keep_ref, send_ref):
    block = lax.axis_index("blk")
    half = lax.axis_size("blk") // 2
    rows, fields = v_ref.shape

    one, two = offset_ref[0], offset_ref[1]
    low, high = jnp.minimum(one, two), jnp.maximum(one, two)
    chained = ring(high - low, half) < ring(high, half)
    plan_ref[0] = low - 1
    plan_ref[1] = jnp.where(chained, half - 1 + high - low, high - 1)
    plan_ref[2] = (two < one).astype(jnp.int32)
    plan_ref[3] = 0

    per_row = fields // rows
    lines, steps = 8, 6
    line, lane = iota((lines, rows), 0), iota((lines, rows), 1)
    pick = jnp.zeros((lines, rows), jnp.float32)
    for s in range(steps):
        mine = block_ref[s // 3, s % 3] == block
        wanted = jnp.where(mine, row_ref[s // 3, s % 3], -1)
        pick = jnp.where((line == s) & (lane == wanted), 1.0, pick)
    held = jnp.broadcast_to(norms_ref[...].astype(jnp.float32), (lines, rows))
    held = jnp.where(line == steps + block // per_row, held, 0.0)
    place = iota((rows, fields), 1) - block % per_row * rows
    spots = jnp.where(place == iota((rows, fields), 0), 1.0, 0.0).astype(jnp.bfloat16)
    total = jnp.dot(pick.astype(jnp.bfloat16), v_ref[...], preferred_element_type=jnp.float32)
    total += jnp.dot(held.astype(jnp.bfloat16), spots, preferred_element_type=jnp.float32)
    left, right = total[:, : fields // 2], total[:, fields // 2 :]
    odd = block % 2 == 1
    keep_ref[...] = jnp.where(odd, right, left).astype(jnp.bfloat16)
    send_ref[...] = jnp.where(odd, left, right).astype(jnp.bfloat16)


def tiles_kernel(plan_ref, v_ref, first_ref, second_ref, got_ref, out_ref, table_ref):
    slices, lines, cols = out_ref.shape
    cols = cols // NOFF
    rows, fields = v_ref.shape
    swap = plan_ref[2] == 1
    got = [got_ref[n].astype(jnp.float32) for n in range(4)]
    every = jnp.concatenate([got[0] + got[2], got[1] + got[3]], axis=1)
    for r in range(2):
        for q in range(fields // 128):
            at = r * (fields // 128) + q
            table_ref[at : at + 1] = every[6 + r : 7 + r, q * 128 : (q + 1) * 128]
    vectors = v_ref[...].astype(jnp.float32)
    found = []
    for partner_ref, t in ((first_ref, 0), (second_ref, 1)):
        scaled = []
        for s in range(3):
            one, other = every[3 * t + s], every[3 * (1 - t) + s]
            pivot = jnp.where(swap, other, one)
            scaled.append((vectors * pivot[None, :]).astype(jnp.bfloat16))
        sums = lax.dot_general(
            jnp.concatenate(scaled, 0),
            partner_ref[...],
            (((1,), (1,)), ((), ())),
            preferred_element_type=jnp.float32,
        )
        found.append(sums.reshape(3, slices, rows // slices, cols))
    ordered = jnp.concatenate(
        [jnp.where(swap, found[1], found[0]), jnp.where(swap, found[0], found[1])], 3
    )
    ordered = jnp.transpose(ordered, (1, 0, 2, 3))
    out_ref[...] = ordered.reshape(slices, lines, NOFF * cols).astype(jnp.bfloat16)


def finish_kernel(offset_ref, block_ref, row_ref, got_ref, norms_ref, table_ref, out_ref):
    block, place = lax.axis_index("blk"), lax.axis_index("fld")
    slices, lines, cols = got_ref.shape
    cols = cols // NOFF
    share = cols // slices
    total = got_ref[0].astype(jnp.float32)
    for n in range(1, slices):
        total += got_ref[n].astype(jnp.float32)
    table = table_ref[...]
    row, lane = iota(table.shape, 0), iota(table.shape, 1)
    entry = row * table.shape[1] + lane
    held = jnp.broadcast_to(norms_ref[...].astype(jnp.float32), (share, cols))
    at = iota((share, cols), 1) == iota((share, cols), 0) + place * share
    own = jnp.sum(jnp.where(at, held, 0.0), axis=1, keepdims=True)
    blocks = table.size // cols
    for t in range(NOFF):
        partner = (block + offset_ref[t]) % blocks
        both = jnp.sum(jnp.where(row == partner // 2, table, 0.0), axis=0, keepdims=True)
        partner_norms = jnp.where(partner % 2 == 1, both[:, cols:], both[:, :cols])
        for s in range(3):
            wanted = block_ref[t, s] * cols + row_ref[t, s]
            pivot = jnp.where(entry == wanted, table, 0.0)
            pivot_norm = jnp.sum(jnp.sum(pivot, axis=0, keepdims=True), axis=1, keepdims=True)
            tile = total[s * share : (s + 1) * share, t * cols : (t + 1) * cols]
            out_ref[t, s] = (tile / ((own * pivot_norm) * partner_norms)).astype(jnp.bfloat16)


def exchange(parts, kind):
    return lax.all_to_all(parts, "blk", 0, 0, axis_index_groups=blk_groups(kind))


def total_of(got, copies):
    total = got.astype(jnp.float32).sum(0).astype(jnp.bfloat16)
    return jnp.broadcast_to(total[None], (copies,) + total.shape)


def shifted(value, by):
    peers = lax.axis_size("blk")
    if by == 0:
        return value
    return lax.ppermute(value, "blk", [(i, (i - by) % peers) for i in range(peers)])


def body(vectors, norms, offsets, pivot_block, pivot_row):
    rows, fields = vectors.shape
    blocks = lax.axis_size("blk")
    slices = lax.axis_size("fld")
    share = rows // slices
    count_piv = pivot_block.shape[1]
    near, along = len(blk_groups("near")[0]), len(blk_groups("z")[0])
    half = blocks // 2
    norms_row = norms.reshape(1, rows)

    lines = jax.ShapeDtypeStruct((8, fields // 2), jnp.bfloat16)
    plan, keep, send = pl.pallas_call(
        prepare_kernel,
        out_shape=(jax.ShapeDtypeStruct((4,), jnp.int32), lines, lines),
        in_specs=[SMEM, SMEM, SMEM, VMEM, VMEM],
        out_specs=(SMEM, VMEM, VMEM),
    )(offsets, pivot_block, pivot_row, vectors, norms_row)
    got = keep + lax.ppermute(send, "blk", [(i, i ^ 1) for i in range(blocks)])
    got = exchange(jnp.broadcast_to(got[None], (along,) + got.shape), "z")

    def pull(source, by):
        return lambda operands: shifted(operands[source], by)

    first = lax.switch(plan[0], [pull(0, k) for k in range(1, half)], (vectors,))
    got, first = lax.optimization_barrier((got, first))
    got = exchange(total_of(got, near), "near")

    direct = [pull(0, k) for k in range(1, half)]
    chained = [pull(1, k) for k in range(half - 1)]
    second = lax.switch(plan[1], direct + chained, (vectors, first))

    sums, table = pl.pallas_call(
        tiles_kernel,
        out_shape=(
            jax.ShapeDtypeStruct((slices, count_piv * share, NOFF * rows), jnp.bfloat16),
            jax.ShapeDtypeStruct((blocks * rows // 128, 128), jnp.float32),
        ),
        in_specs=[SMEM, VMEM, VMEM, VMEM, VMEM],
        out_specs=(VMEM, VMEM),
        compiler_params=SMALL,
    )(plan, vectors, first, second, got)
    got = lax.all_to_all(sums, "fld", 0, 0)

    return pl.pallas_call(
        finish_kernel,
        out_shape=jax.ShapeDtypeStruct((NOFF, count_piv, share, rows), jnp.bfloat16),
        in_specs=[SMEM, SMEM, SMEM, VMEM, VMEM, VMEM],
        out_specs=VMEM,
        compiler_params=SMALL,
    )(offsets, pivot_block, pivot_row, got, norms_row, table)


def solution(mesh):
    return jax.shard_map(
        body,
        mesh=mesh,
        in_specs=(P("blk", "fld"), P("blk"), P(), P(), P()),
        out_specs=P(None, None, ("blk", "fld"), None),
        check_vma=False,
    )
```

```python
import jax
import jax.numpy as jnp
from jax import lax
from jax.experimental import pallas as pl
from jax.experimental.pallas import tpu as pltpu
from jax.sharding import PartitionSpec as P

NOFF = 2
VMEM = pl.BlockSpec(memory_space=pltpu.VMEM)
SMEM = pl.BlockSpec(memory_space=pltpu.SMEM)
SMALL = pltpu.CompilerParams(vmem_limit_bytes=16 * 2**20)


def blk_groups(kind):
    at = lambda y, z, c: (y * 16 + z) * 2 + c
    if kind == "near":
        return [[at(y, z, c) for y in range(2) for c in range(2)] for z in range(16)]
    return [[at(y, z, c) for z in range(16)] for y in range(2) for c in range(2)]


def iota(shape, dim):
    return lax.broadcasted_iota(jnp.int32, shape, dim)


def ring(k, half):
    return jnp.minimum(k % half, half - k % half)


def prepare_kernel(offset_ref, block_ref, row_ref, v_ref, norms_ref, one_ref, two_ref, swap_ref, out_ref):
    block = lax.axis_index("blk")
    half = lax.axis_size("blk") // 2
    rows, fields = v_ref.shape

    one, two = offset_ref[0], offset_ref[1]
    low, high = jnp.minimum(one, two), jnp.maximum(one, two)
    chained = ring(high - low, half) < ring(high, half)
    one_ref[0] = low - 1
    two_ref[0] = jnp.where(chained, half - 1 + high - low, high - 1)
    swap_ref[0] = (two < one).astype(jnp.int32)

    lines, steps = 8, 6
    line, lane = iota((lines, rows), 0), iota((lines, rows), 1)
    pick = jnp.zeros((lines, rows), jnp.float32)
    for s in range(steps):
        mine = block_ref[s // 3, s % 3] == block
        wanted = jnp.where(mine, row_ref[s // 3, s % 3], -1)
        pick = jnp.where((line == s) & (lane == wanted), 1.0, pick)
    total = jnp.dot(pick.astype(jnp.bfloat16), v_ref[...], preferred_element_type=jnp.float32)
    member = block // half * 2 + block % 2
    held = jnp.concatenate([norms_ref[...].astype(jnp.float32)] * 2, axis=1)
    row, lane = iota((2, 128), 0), iota((2, 128), 1)
    held = jnp.where((row == member // 2) & (lane // rows == member % 2), held, 0.0)
    parts = out_ref.shape[0]
    for n in range(parts):
        for q in range(4):
            at = n % 2 * (fields // 2) + q * 256
            pair = [total[:steps, at : at + 128], total[:steps, at + 128 : at + 256]]
            out_ref[n, q * steps : (q + 1) * steps] = jnp.stack(pair, 1).astype(jnp.bfloat16)
        out_ref[n, 4 * steps] = held.astype(jnp.bfloat16)


def tiles_kernel(swap_ref, v_ref, first_ref, second_ref, mine_ref, other_ref, out_ref):
    slices, lines, cols = out_ref.shape
    cols = cols // NOFF
    rows, fields = v_ref.shape
    swap = swap_ref[0] == 1
    odd = lax.axis_index("blk") % 2 == 1
    mine, other = mine_ref[...].astype(jnp.float32), other_ref[...].astype(jnp.float32)
    halves = (jnp.where(odd, other, mine), jnp.where(odd, mine, other))
    every = [
        jnp.concatenate([h[q * 6 + s, n : n + 1] for h in halves for q in range(4) for n in range(2)], axis=1)
        for s in range(6)
    ]
    vectors = v_ref[...]
    found = []
    for partner_ref, t in ((first_ref, 0), (second_ref, 1)):
        scaled = []
        for s in range(3):
            one, other = every[3 * t + s], every[3 * (1 - t) + s]
            pivot = jnp.where(swap, other, one)
            scaled.append(vectors * pivot.astype(jnp.bfloat16))
        sums = lax.dot_general(
            jnp.concatenate(scaled, 0),
            partner_ref[...],
            (((1,), (1,)), ((), ())),
            preferred_element_type=jnp.float32,
        )
        found.append(sums.reshape(3, slices, rows // slices, cols))
    ordered = jnp.concatenate(
        [jnp.where(swap, found[1], found[0]), jnp.where(swap, found[0], found[1])], 3
    )
    ordered = jnp.transpose(ordered, (1, 0, 2, 3))
    out_ref[...] = ordered.reshape(slices, lines, NOFF * cols).astype(jnp.bfloat16)


def finish_kernel(offset_ref, block_ref, row_ref, got_ref, norms_ref, table_ref, out_ref):
    block, place = lax.axis_index("blk"), lax.axis_index("fld")
    slices, lines, cols = got_ref.shape
    cols = cols // NOFF
    share = cols // slices
    total = got_ref[0].astype(jnp.float32)
    for n in range(1, slices):
        total += got_ref[n].astype(jnp.float32)
    table = table_ref[...].astype(jnp.float32)
    row, lane = iota(table.shape, 0), iota(table.shape, 1)
    entry = row * table.shape[1] + lane
    held = jnp.broadcast_to(norms_ref[...].astype(jnp.float32), (share, cols))
    at = iota((share, cols), 1) == iota((share, cols), 0) + place * share
    own = jnp.sum(jnp.where(at, held, 0.0), axis=1, keepdims=True)
    blocks = table.size // cols
    line_of = lambda b: b // 2 % (blocks // 4) * 2 + b // (blocks // 2)
    for t in range(NOFF):
        partner = (block + offset_ref[t]) % blocks
        both = jnp.sum(jnp.where(row == line_of(partner), table, 0.0), axis=0, keepdims=True)
        partner_norms = jnp.where(partner % 2 == 1, both[:, cols:], both[:, :cols])
        for s in range(3):
            owner = block_ref[t, s]
            wanted = (line_of(owner) * 2 + owner % 2) * cols + row_ref[t, s]
            pivot = jnp.where(entry == wanted, table, 0.0)
            pivot_norm = jnp.sum(jnp.sum(pivot, axis=0, keepdims=True), axis=1, keepdims=True)
            tile = total[s * share : (s + 1) * share, t * cols : (t + 1) * cols]
            out_ref[t, s] = (tile / ((own * pivot_norm) * partner_norms)).astype(jnp.bfloat16)


def exchange(parts, kind):
    return lax.all_to_all(parts, "blk", 0, 0, axis_index_groups=blk_groups(kind))


def total_of(got, copies):
    total = got.astype(jnp.float32).sum(0).astype(jnp.bfloat16)
    return jnp.broadcast_to(total[None], (copies,) + total.shape)


def shifted(value, by):
    peers = lax.axis_size("blk")
    if by == 0:
        return value
    return lax.ppermute(value, "blk", [(i, (i - by) % peers) for i in range(peers)])


def body(vectors, norms, offsets, pivot_block, pivot_row):
    rows, fields = vectors.shape
    blocks = lax.axis_size("blk")
    slices = lax.axis_size("fld")
    share = rows // slices
    count_piv = pivot_block.shape[1]
    near, along = len(blk_groups("near")[0]), len(blk_groups("z")[0])
    half = blocks // 2
    norms_row = norms.reshape(1, rows)

    word = jax.ShapeDtypeStruct((1,), jnp.int32)
    lines = jax.ShapeDtypeStruct((near, 25, 2, 128), jnp.bfloat16)
    plan_one, plan_two, swap, parts = pl.pallas_call(
        prepare_kernel,
        out_shape=(word, word, word, lines),
        in_specs=[SMEM, SMEM, SMEM, VMEM, VMEM],
        out_specs=(SMEM, SMEM, SMEM, VMEM),
    )(offsets, pivot_block, pivot_row, vectors, norms_row)
    def pull(source, by):
        return lambda operands: shifted(operands[source], by)

    got = exchange(parts, "near")
    first = lax.switch(plan_one[0], [pull(0, k) for k in range(1, half)], (vectors,))
    got, first = lax.optimization_barrier((got, first))
    got = exchange(total_of(got, along), "z")

    direct = [pull(0, k) for k in range(1, half)]
    chained = [pull(1, k) for k in range(half - 1)]
    second = lax.switch(plan_two[0], direct + chained, (vectors, first))
    got, second = lax.optimization_barrier((got, second))
    mine = got[:, :-1].astype(jnp.float32).sum(0).astype(jnp.bfloat16)
    table = got[:, -1].reshape(blocks // 2, 2 * rows)
    other = lax.ppermute(mine, "blk", [(i, i ^ 1) for i in range(blocks)])

    sums = pl.pallas_call(
        tiles_kernel,
        out_shape=jax.ShapeDtypeStruct((slices, count_piv * share, NOFF * rows), jnp.bfloat16),
        in_specs=[SMEM] + [VMEM] * 5,
        out_specs=VMEM,
        compiler_params=SMALL,
    )(swap, vectors, first, second, mine, other)
    got = lax.all_to_all(sums, "fld", 0, 0)

    return pl.pallas_call(
        finish_kernel,
        out_shape=jax.ShapeDtypeStruct((NOFF, count_piv, share, rows), jnp.bfloat16),
        in_specs=[SMEM, SMEM, SMEM, VMEM, VMEM, VMEM],
        out_specs=VMEM,
        compiler_params=SMALL,
    )(offsets, pivot_block, pivot_row, got, norms_row, table)


def solution(mesh):
    return jax.shard_map(
        body,
        mesh=mesh,
        in_specs=(P("blk", "fld"), P("blk"), P(), P(), P()),
        out_specs=P(None, None, ("blk", "fld"), None),
        check_vma=False,
    )
```

```python
import jax
import jax.numpy as jnp
from jax import lax
from jax.experimental import pallas as pl
from jax.experimental.pallas import tpu as pltpu
from jax.sharding import PartitionSpec as P

NOFF = 2
CLOSE = 2
VMEM = pl.BlockSpec(memory_space=pltpu.VMEM)
SMEM = pl.BlockSpec(memory_space=pltpu.SMEM)
SMALL = pltpu.CompilerParams(vmem_limit_bytes=16 * 2**20)


def blk_groups(kind):
    at = lambda y, z, c: (y * 16 + z) * 2 + c
    if kind == "close":
        return [
            [at(y, CLOSE * far + z, c) for z in range(CLOSE) for y in range(2) for c in range(2)]
            for far in range(16 // CLOSE)
        ]
    return [
        [at(y, CLOSE * far + z, c) for far in range(16 // CLOSE)]
        for z in range(CLOSE)
        for y in range(2)
        for c in range(2)
    ]


def iota(shape, dim):
    return lax.broadcasted_iota(jnp.int32, shape, dim)


def prepare_kernel(offset_ref, block_ref, row_ref, v_ref, norms_ref, one_ref, two_ref, swap_ref, out_ref):
    block = lax.axis_index("blk")
    half = lax.axis_size("blk") // 2
    rows, fields = v_ref.shape

    one, two = offset_ref[0], offset_ref[1]
    low, high = jnp.minimum(one, two), jnp.maximum(one, two)
    gap = high - low
    chained = (high <= half // 2) | (gap < half - high)
    one_ref[0] = low - 1
    two_ref[0] = jnp.where(chained, gap, high - 1)
    swap_ref[0] = (two < one).astype(jnp.int32)

    lines, steps = 8, 6
    line, lane = iota((lines, rows), 0), iota((lines, rows), 1)
    pick = jnp.zeros((lines, rows), jnp.float32)
    for s in range(steps):
        mine = block_ref[s // 3, s % 3] == block
        wanted = jnp.where(mine, row_ref[s // 3, s % 3], -1)
        pick = jnp.where((line == s) & (lane == wanted), 1.0, pick)
    total = jnp.dot(pick.astype(jnp.bfloat16), v_ref[...], preferred_element_type=jnp.float32)
    mine = block // 2 % CLOSE * 2 + block // half
    held = jnp.concatenate([norms_ref[...].astype(jnp.float32)] * 2, axis=1)
    row, lane = iota((2, 128), 0), iota((2, 128), 1)
    held = jnp.where(lane // rows == block % 2, held, 0.0)
    parts = out_ref.shape[0]
    for n in range(parts):
        for q in range(4 * steps):
            at = n % 2 * (fields // 2) + q // 3 * 128
            pair = total[q % 3 * 2 : q % 3 * 2 + 2, at : at + 128]
            out_ref[n, q] = pair.astype(jnp.bfloat16)
        for q in range(CLOSE):
            out_ref[n, 4 * steps + q] = jnp.where(2 * q + row == mine, held, 0.0).astype(jnp.bfloat16)


def tiles_kernel(swap_ref, v_ref, first_ref, second_ref, mine_ref, other_ref, out_ref):
    slices, lines, cols = out_ref.shape
    cols = cols // NOFF
    rows, fields = v_ref.shape
    odd = lax.axis_index("blk") % 2 == 1
    mine, other = mine_ref[...].astype(jnp.float32), other_ref[...].astype(jnp.float32)
    halves = (jnp.where(odd, other, mine), jnp.where(odd, mine, other))
    vectors = v_ref[...]

    def tiles(partners):
        found = []
        for t, partner_ref in enumerate(partners):
            scaled = []
            for s in range(3 * t, 3 * t + 3):
                parts = [h[q * 3 + s // 2, s % 2 : s % 2 + 1] for h in halves for q in range(8)]
                scaled.append(vectors * jnp.concatenate(parts, axis=1).astype(jnp.bfloat16))
            sums = lax.dot_general(
                jnp.concatenate(scaled, 0),
                partner_ref[...],
                (((1,), (1,)), ((), ())),
                preferred_element_type=jnp.float32,
            )
            found.append(sums.reshape(3, slices, rows // slices, cols))
        ordered = jnp.transpose(jnp.concatenate(found, 3), (1, 0, 2, 3))
        out_ref[...] = ordered.reshape(slices, lines, NOFF * cols).astype(jnp.bfloat16)

    @pl.when(swap_ref[0] == 0)
    def _():
        tiles((first_ref, second_ref))

    @pl.when(swap_ref[0] == 1)
    def _():
        tiles((second_ref, first_ref))


def finish_kernel(offset_ref, block_ref, row_ref, got_ref, norms_ref, lines_ref, out_ref):
    block, place = lax.axis_index("blk"), lax.axis_index("fld")
    slices, lines, cols = got_ref.shape
    cols = cols // NOFF
    share = cols // slices
    total = got_ref[0].astype(jnp.float32)
    for n in range(1, slices):
        total += got_ref[n].astype(jnp.float32)
    table = lines_ref[:, lines_ref.shape[1] - CLOSE :].astype(jnp.float32)
    line = (iota(table.shape, 0) * CLOSE + iota(table.shape, 1)) * 2 + iota(table.shape, 2)
    lane = iota(table.shape, 3)
    held = jnp.broadcast_to(norms_ref[...].astype(jnp.float32), (share, cols))
    at = iota((share, cols), 1) == iota((share, cols), 0) + place * share
    own = jnp.sum(jnp.where(at, held, 0.0), axis=1, keepdims=True)
    blocks = table.size // cols
    line_of = lambda b: b // 2 % (blocks // 4) * 2 + b // (blocks // 2)
    picked = lambda where: jnp.sum(jnp.where(where, table, 0.0), axis=(0, 1, 2)).reshape(1, 2 * cols)
    for t in range(NOFF):
        partner = (block + offset_ref[t]) % blocks
        both = picked(line == line_of(partner))
        partner_norms = jnp.where(partner % 2 == 1, both[:, cols:], both[:, :cols])
        for s in range(3):
            owner = block_ref[t, s]
            at = owner % 2 * cols + row_ref[t, s]
            pivot_norm = jnp.sum(picked((line == line_of(owner)) & (lane == at)), axis=1, keepdims=True)
            tile = total[s * share : (s + 1) * share, t * cols : (t + 1) * cols]
            out_ref[t, s] = (tile / ((own * pivot_norm) * partner_norms)).astype(jnp.bfloat16)


def exchange(parts, kind):
    return lax.all_to_all(parts, "blk", 0, 0, axis_index_groups=blk_groups(kind))


def total_of(got, copies):
    total = got.astype(jnp.float32).sum(0).astype(jnp.bfloat16)
    return jnp.broadcast_to(total[None], (copies,) + total.shape)


def shifted(value, by):
    peers = lax.axis_size("blk")
    if by == 0:
        return value
    return lax.ppermute(value, "blk", [(i, (i - by) % peers) for i in range(peers)])


def body(vectors, norms, offsets, pivot_block, pivot_row):
    rows, fields = vectors.shape
    blocks = lax.axis_size("blk")
    slices = lax.axis_size("fld")
    share = rows // slices
    count_piv = pivot_block.shape[1]
    close, far = len(blk_groups("close")[0]), len(blk_groups("far")[0])
    half = blocks // 2
    norms_row = norms.reshape(1, rows)

    word = jax.ShapeDtypeStruct((1,), jnp.int32)
    lines = jax.ShapeDtypeStruct((close, 24 + CLOSE, 2, 128), jnp.bfloat16)
    plan_one, plan_two, swap, parts = pl.pallas_call(
        prepare_kernel,
        out_shape=(word, word, word, lines),
        in_specs=[SMEM, SMEM, SMEM, VMEM, VMEM],
        out_specs=(SMEM, SMEM, SMEM, VMEM),
    )(offsets, pivot_block, pivot_row, vectors, norms_row)
    def pull(source, by):
        return lambda operands: shifted(operands[source], by)

    got = exchange(parts, "close")
    first = lax.switch(plan_one[0], [pull(0, k) for k in range(1, half)], (vectors,))
    got, first = lax.optimization_barrier((got, first))
    got = exchange(total_of(got, far), "far")

    chained = [pull(1, k) for k in range(half // 2)]
    direct = [pull(0, k) for k in range(half // 2 + 1, half)]
    second = lax.switch(plan_two[0], chained + direct, (vectors, first))
    got, second = lax.optimization_barrier((got, second))
    mine = got[:, :24].astype(jnp.float32).sum(0).astype(jnp.bfloat16)
    lines = got
    other = lax.ppermute(mine, "blk", [(i, i ^ 1) for i in range(blocks)])

    sums = pl.pallas_call(
        tiles_kernel,
        out_shape=jax.ShapeDtypeStruct((slices, count_piv * share, NOFF * rows), jnp.bfloat16),
        in_specs=[SMEM] + [VMEM] * 5,
        out_specs=VMEM,
        compiler_params=SMALL,
    )(swap, vectors, first, second, mine, other)
    got = lax.all_to_all(sums, "fld", 0, 0)

    return pl.pallas_call(
        finish_kernel,
        out_shape=jax.ShapeDtypeStruct((NOFF, count_piv, share, rows), jnp.bfloat16),
        in_specs=[SMEM, SMEM, SMEM, VMEM, VMEM, VMEM],
        out_specs=VMEM,
        compiler_params=SMALL,
    )(offsets, pivot_block, pivot_row, got, norms_row, lines)


def solution(mesh):
    return jax.shard_map(
        body,
        mesh=mesh,
        in_specs=(P("blk", "fld"), P("blk"), P(), P(), P()),
        out_specs=P(None, None, ("blk", "fld"), None),
        check_vma=False,
    )
```

```python
import jax
import jax.numpy as jnp
from jax import lax
from jax.experimental import pallas as pl
from jax.experimental.pallas import tpu as pltpu
from jax.sharding import PartitionSpec as P

NOFF = 2
CLOSE = 2
MOVE, COVER = 1, 4
VMEM = pl.BlockSpec(memory_space=pltpu.VMEM)
SMEM = pl.BlockSpec(memory_space=pltpu.SMEM)
SMALL = pltpu.CompilerParams(vmem_limit_bytes=16 * 2**20)


def blk_groups(kind):
    at = lambda y, z, c: (y * 16 + z) * 2 + c
    if kind == "close":
        return [
            [at(y, CLOSE * far + z, c) for z in range(CLOSE) for y in range(2) for c in range(2)]
            for far in range(16 // CLOSE)
        ]
    return [
        [at(y, CLOSE * far + z, c) for far in range(16 // CLOSE)]
        for z in range(CLOSE)
        for y in range(2)
        for c in range(2)
    ]


def iota(shape, dim):
    return lax.broadcasted_iota(jnp.int32, shape, dim)


def prepare_kernel(offset_ref, block_ref, row_ref, v_ref, norms_ref, one_ref, two_ref, swap_ref, out_ref):
    block = lax.axis_index("blk")
    half = lax.axis_size("blk") // 2
    rows, fields = v_ref.shape

    one, two = offset_ref[0], offset_ref[1]
    low, high = jnp.minimum(one, two), jnp.maximum(one, two)
    gap = high - low
    near, far = (MOVE + jnp.minimum(k, half - k) for k in (low, high))
    cover = lambda cost: jnp.maximum(cost, COVER)
    chained = half // 2
    lead, then, late = low, gap, 0
    best = jnp.where(gap < chained, near + cover(MOVE + gap), 4 * half)
    for cost, way in (
        (near + cover(far), (low, chained + high - 1, 0)),
        (far + cover(near), (high, chained + low - 1, 1)),
    ):
        take = cost < best
        lead, then, late = (jnp.where(take, new, old) for new, old in zip(way, (lead, then, late)))
        best = jnp.where(take, cost, best)
    one_ref[0] = lead - 1
    two_ref[0] = then
    swap_ref[0] = jnp.where(one < two, late, jnp.where(two < one, 1 - late, 0))

    lines, steps = 8, 6
    line, lane = iota((lines, rows), 0), iota((lines, rows), 1)
    pick = jnp.zeros((lines, rows), jnp.float32)
    for s in range(steps):
        mine = block_ref[s // 3, s % 3] == block
        wanted = jnp.where(mine, row_ref[s // 3, s % 3], -1)
        pick = jnp.where((line == s) & (lane == wanted), 1.0, pick)
    total = jnp.dot(pick.astype(jnp.bfloat16), v_ref[...], preferred_element_type=jnp.float32)
    mine = block // 2 % CLOSE * 2 + block // half
    held = jnp.concatenate([norms_ref[...].astype(jnp.float32)] * 2, axis=1)
    row, lane = iota((2, 128), 0), iota((2, 128), 1)
    held = jnp.where(lane // rows == block % 2, held, 0.0)
    parts = out_ref.shape[0]
    for n in range(parts):
        for q in range(4 * steps):
            at = n % 2 * (fields // 2) + q // 3 * 128
            pair = total[q % 3 * 2 : q % 3 * 2 + 2, at : at + 128]
            out_ref[n, q] = pair.astype(jnp.bfloat16)
        for q in range(CLOSE):
            out_ref[n, 4 * steps + q] = jnp.where(2 * q + row == mine, held, 0.0).astype(jnp.bfloat16)


def tiles_kernel(swap_ref, v_ref, first_ref, second_ref, mine_ref, other_ref, out_ref):
    slices, lines, cols = out_ref.shape
    cols = cols // NOFF
    rows, fields = v_ref.shape
    odd = lax.axis_index("blk") % 2 == 1
    mine, other = mine_ref[...].astype(jnp.float32), other_ref[...].astype(jnp.float32)
    halves = (jnp.where(odd, other, mine), jnp.where(odd, mine, other))
    vectors = v_ref[...]

    def tiles(partners):
        found = []
        for t, partner_ref in enumerate(partners):
            scaled = []
            for s in range(3 * t, 3 * t + 3):
                parts = [h[q * 3 + s // 2, s % 2 : s % 2 + 1] for h in halves for q in range(8)]
                scaled.append(vectors * jnp.concatenate(parts, axis=1).astype(jnp.bfloat16))
            sums = lax.dot_general(
                jnp.concatenate(scaled, 0),
                partner_ref[...],
                (((1,), (1,)), ((), ())),
                preferred_element_type=jnp.float32,
            )
            found.append(sums.reshape(3, slices, rows // slices, cols))
        ordered = jnp.transpose(jnp.concatenate(found, 3), (1, 0, 2, 3))
        out_ref[...] = ordered.reshape(slices, lines, NOFF * cols).astype(jnp.bfloat16)

    @pl.when(swap_ref[0] == 0)
    def _():
        tiles((first_ref, second_ref))

    @pl.when(swap_ref[0] == 1)
    def _():
        tiles((second_ref, first_ref))


def finish_kernel(offset_ref, block_ref, row_ref, got_ref, norms_ref, lines_ref, out_ref):
    block, place = lax.axis_index("blk"), lax.axis_index("fld")
    slices, lines, cols = got_ref.shape
    cols = cols // NOFF
    share = cols // slices
    total = got_ref[0].astype(jnp.float32)
    for n in range(1, slices):
        total += got_ref[n].astype(jnp.float32)
    table = lines_ref[:, lines_ref.shape[1] - CLOSE :].astype(jnp.float32)
    line = (iota(table.shape, 0) * CLOSE + iota(table.shape, 1)) * 2 + iota(table.shape, 2)
    lane = iota(table.shape, 3)
    held = jnp.broadcast_to(norms_ref[...].astype(jnp.float32), (share, cols))
    at = iota((share, cols), 1) == iota((share, cols), 0) + place * share
    own = jnp.sum(jnp.where(at, held, 0.0), axis=1, keepdims=True)
    blocks = table.size // cols
    line_of = lambda b: b // 2 % (blocks // 4) * 2 + b // (blocks // 2)
    picked = lambda where: jnp.sum(jnp.where(where, table, 0.0), axis=(0, 1, 2)).reshape(1, 2 * cols)
    for t in range(NOFF):
        partner = (block + offset_ref[t]) % blocks
        both = picked(line == line_of(partner))
        partner_norms = jnp.where(partner % 2 == 1, both[:, cols:], both[:, :cols])
        for s in range(3):
            owner = block_ref[t, s]
            at = owner % 2 * cols + row_ref[t, s]
            pivot_norm = jnp.sum(picked((line == line_of(owner)) & (lane == at)), axis=1, keepdims=True)
            tile = total[s * share : (s + 1) * share, t * cols : (t + 1) * cols]
            out_ref[t, s] = (tile / ((own * pivot_norm) * partner_norms)).astype(jnp.bfloat16)


def exchange(parts, kind):
    return lax.all_to_all(parts, "blk", 0, 0, axis_index_groups=blk_groups(kind))


def total_of(got, copies):
    total = got.astype(jnp.float32).sum(0).astype(jnp.bfloat16)
    return jnp.broadcast_to(total[None], (copies,) + total.shape)


def shifted(value, by):
    peers = lax.axis_size("blk")
    if by == 0:
        return value
    return lax.ppermute(value, "blk", [(i, (i - by) % peers) for i in range(peers)])


def body(vectors, norms, offsets, pivot_block, pivot_row):
    rows, fields = vectors.shape
    blocks = lax.axis_size("blk")
    slices = lax.axis_size("fld")
    share = rows // slices
    count_piv = pivot_block.shape[1]
    close, far = len(blk_groups("close")[0]), len(blk_groups("far")[0])
    half = blocks // 2
    norms_row = norms.reshape(1, rows)

    word = jax.ShapeDtypeStruct((1,), jnp.int32)
    lines = jax.ShapeDtypeStruct((close, 24 + CLOSE, 2, 128), jnp.bfloat16)
    plan_one, plan_two, swap, parts = pl.pallas_call(
        prepare_kernel,
        out_shape=(word, word, word, lines),
        in_specs=[SMEM, SMEM, SMEM, VMEM, VMEM],
        out_specs=(SMEM, SMEM, SMEM, VMEM),
    )(offsets, pivot_block, pivot_row, vectors, norms_row)
    def pull(source, by):
        return lambda operands: shifted(operands[source], by)

    got = exchange(parts, "close")
    first = lax.switch(plan_one[0], [pull(0, k) for k in range(1, half)], (vectors,))
    got, first = lax.optimization_barrier((got, first))
    got = exchange(total_of(got, far), "far")

    chained = [pull(1, k) for k in range(half // 2)]
    direct = [pull(0, k) for k in range(1, half)]
    second = lax.switch(plan_two[0], chained + direct, (vectors, first))
    got, second = lax.optimization_barrier((got, second))
    mine = got[:, :24].astype(jnp.float32).sum(0).astype(jnp.bfloat16)
    lines = got
    other = lax.ppermute(mine, "blk", [(i, i ^ 1) for i in range(blocks)])

    sums = pl.pallas_call(
        tiles_kernel,
        out_shape=jax.ShapeDtypeStruct((slices, count_piv * share, NOFF * rows), jnp.bfloat16),
        in_specs=[SMEM] + [VMEM] * 5,
        out_specs=VMEM,
        compiler_params=SMALL,
    )(swap, vectors, first, second, mine, other)
    got = lax.all_to_all(sums, "fld", 0, 0)

    return pl.pallas_call(
        finish_kernel,
        out_shape=jax.ShapeDtypeStruct((NOFF, count_piv, share, rows), jnp.bfloat16),
        in_specs=[SMEM, SMEM, SMEM, VMEM, VMEM, VMEM],
        out_specs=VMEM,
        compiler_params=SMALL,
    )(offsets, pivot_block, pivot_row, got, norms_row, lines)


def solution(mesh):
    return jax.shard_map(
        body,
        mesh=mesh,
        in_specs=(P("blk", "fld"), P("blk"), P(), P(), P()),
        out_specs=P(None, None, ("blk", "fld"), None),
        check_vma=False,
    )
```

```python
import jax
import jax.numpy as jnp
from jax import lax
from jax.experimental import pallas as pl
from jax.experimental.pallas import tpu as pltpu
from jax.sharding import PartitionSpec as P

NOFF = 2
CLOSE = 2
MOVE, COVER = 1, 3
VMEM = pl.BlockSpec(memory_space=pltpu.VMEM)
SMEM = pl.BlockSpec(memory_space=pltpu.SMEM)
SMALL = pltpu.CompilerParams(vmem_limit_bytes=16 * 2**20)


def blk_groups(kind):
    at = lambda y, z, c: (y * 16 + z) * 2 + c
    if kind == "close":
        return [
            [at(y, CLOSE * far + z, c) for z in range(CLOSE) for y in range(2) for c in range(2)]
            for far in range(16 // CLOSE)
        ]
    return [
        [at(y, CLOSE * far + z, c) for far in range(16 // CLOSE)]
        for z in range(CLOSE)
        for y in range(2)
        for c in range(2)
    ]


def iota(shape, dim):
    return lax.broadcasted_iota(jnp.int32, shape, dim)


def prepare_kernel(offset_ref, block_ref, row_ref, v_ref, norms_ref, one_ref, two_ref, swap_ref, out_ref):
    block = lax.axis_index("blk")
    half = lax.axis_size("blk") // 2
    rows, fields = v_ref.shape

    one, two = offset_ref[0], offset_ref[1]
    low, high = jnp.minimum(one, two), jnp.maximum(one, two)
    gap = high - low
    near, far = (MOVE + jnp.minimum(k, half - k) for k in (low, high))
    cover = lambda cost: jnp.maximum(cost, COVER)
    chained = half // 2
    lead, then, late = low, gap, 0
    best = jnp.where(gap < chained, near + cover(MOVE + gap), 4 * half)
    for cost, way in (
        (near + cover(far), (low, chained + high - 1, 0)),
        (far + cover(near), (high, chained + low - 1, 1)),
    ):
        take = cost < best
        lead, then, late = (jnp.where(take, new, old) for new, old in zip(way, (lead, then, late)))
        best = jnp.where(take, cost, best)
    one_ref[0] = lead - 1
    two_ref[0] = then
    swap_ref[0] = jnp.where(one < two, late, jnp.where(two < one, 1 - late, 0))

    lines, steps = 8, 6
    line, lane = iota((lines, rows), 0), iota((lines, rows), 1)
    pick = jnp.zeros((lines, rows), jnp.float32)
    for s in range(steps):
        mine = block_ref[s // 3, s % 3] == block
        wanted = jnp.where(mine, row_ref[s // 3, s % 3], -1)
        pick = jnp.where((line == s) & (lane == wanted), 1.0, pick)
    total = jnp.dot(pick.astype(jnp.bfloat16), v_ref[...], preferred_element_type=jnp.float32)
    mine = block // 2 % CLOSE * 2 + block // half
    held = jnp.concatenate([norms_ref[...].astype(jnp.float32)] * 2, axis=1)
    row, lane = iota((2, 128), 0), iota((2, 128), 1)
    held = jnp.where(lane // rows == block % 2, held, 0.0)
    parts = out_ref.shape[0]
    for n in range(parts):
        for q in range(4 * steps):
            at = n % 2 * (fields // 2) + q // 3 * 128
            pair = total[q % 3 * 2 : q % 3 * 2 + 2, at : at + 128]
            out_ref[n, q] = pair.astype(jnp.bfloat16)
        for q in range(CLOSE):
            out_ref[n, 4 * steps + q] = jnp.where(2 * q + row == mine, held, 0.0).astype(jnp.bfloat16)


def tiles_kernel(swap_ref, v_ref, first_ref, second_ref, mine_ref, other_ref, out_ref):
    slices, lines, cols = out_ref.shape
    cols = cols // NOFF
    rows, fields = v_ref.shape
    odd = lax.axis_index("blk") % 2 == 1
    mine, other = mine_ref[...].astype(jnp.float32), other_ref[...].astype(jnp.float32)
    halves = (jnp.where(odd, other, mine), jnp.where(odd, mine, other))
    vectors = v_ref[...]

    def tiles(partners):
        found = []
        for t, partner_ref in enumerate(partners):
            scaled = []
            for s in range(3 * t, 3 * t + 3):
                parts = [h[q * 3 + s // 2, s % 2 : s % 2 + 1] for h in halves for q in range(8)]
                scaled.append(vectors * jnp.concatenate(parts, axis=1).astype(jnp.bfloat16))
            sums = lax.dot_general(
                jnp.concatenate(scaled, 0),
                partner_ref[...],
                (((1,), (1,)), ((), ())),
                preferred_element_type=jnp.float32,
            )
            found.append(sums.reshape(3, slices, rows // slices, cols))
        ordered = jnp.transpose(jnp.concatenate(found, 3), (1, 0, 2, 3))
        out_ref[...] = ordered.reshape(slices, lines, NOFF * cols).astype(jnp.bfloat16)

    @pl.when(swap_ref[0] == 0)
    def _():
        tiles((first_ref, second_ref))

    @pl.when(swap_ref[0] == 1)
    def _():
        tiles((second_ref, first_ref))


def finish_kernel(offset_ref, block_ref, row_ref, got_ref, norms_ref, lines_ref, out_ref):
    block, place = lax.axis_index("blk"), lax.axis_index("fld")
    slices, lines, cols = got_ref.shape
    cols = cols // NOFF
    share = cols // slices
    total = got_ref[0].astype(jnp.float32)
    for n in range(1, slices):
        total += got_ref[n].astype(jnp.float32)
    table = lines_ref[:, lines_ref.shape[1] - CLOSE :].astype(jnp.float32)
    line = (iota(table.shape, 0) * CLOSE + iota(table.shape, 1)) * 2 + iota(table.shape, 2)
    lane = iota(table.shape, 3)
    held = jnp.broadcast_to(norms_ref[...].astype(jnp.float32), (share, cols))
    at = iota((share, cols), 1) == iota((share, cols), 0) + place * share
    own = jnp.sum(jnp.where(at, held, 0.0), axis=1, keepdims=True)
    blocks = table.size // cols
    line_of = lambda b: b // 2 % (blocks // 4) * 2 + b // (blocks // 2)
    picked = lambda where: jnp.sum(jnp.where(where, table, 0.0), axis=(0, 1, 2)).reshape(1, 2 * cols)
    for t in range(NOFF):
        partner = (block + offset_ref[t]) % blocks
        both = picked(line == line_of(partner))
        partner_norms = jnp.where(partner % 2 == 1, both[:, cols:], both[:, :cols])
        for s in range(3):
            owner = block_ref[t, s]
            at = owner % 2 * cols + row_ref[t, s]
            pivot_norm = jnp.sum(picked((line == line_of(owner)) & (lane == at)), axis=1, keepdims=True)
            tile = total[s * share : (s + 1) * share, t * cols : (t + 1) * cols]
            out_ref[t, s] = (tile / ((own * pivot_norm) * partner_norms)).astype(jnp.bfloat16)


def exchange(parts, kind):
    return lax.all_to_all(parts, "blk", 0, 0, axis_index_groups=blk_groups(kind))


def total_of(got, copies):
    total = got.astype(jnp.float32).sum(0).astype(jnp.bfloat16)
    return jnp.broadcast_to(total[None], (copies,) + total.shape)


def shifted(value, by):
    peers = lax.axis_size("blk")
    if by == 0:
        return value
    return lax.ppermute(value, "blk", [(i, (i - by) % peers) for i in range(peers)])


def body(vectors, norms, offsets, pivot_block, pivot_row):
    rows, fields = vectors.shape
    blocks = lax.axis_size("blk")
    slices = lax.axis_size("fld")
    share = rows // slices
    count_piv = pivot_block.shape[1]
    close, far = len(blk_groups("close")[0]), len(blk_groups("far")[0])
    half = blocks // 2
    norms_row = norms.reshape(1, rows)

    word = jax.ShapeDtypeStruct((1,), jnp.int32)
    lines = jax.ShapeDtypeStruct((close, 24 + CLOSE, 2, 128), jnp.bfloat16)
    plan_one, plan_two, swap, parts = pl.pallas_call(
        prepare_kernel,
        out_shape=(word, word, word, lines),
        in_specs=[SMEM, SMEM, SMEM, VMEM, VMEM],
        out_specs=(SMEM, SMEM, SMEM, VMEM),
    )(offsets, pivot_block, pivot_row, vectors, norms_row)
    def pull(source, by):
        return lambda operands: shifted(operands[source], by)

    got = exchange(parts, "close")
    first = lax.switch(plan_one[0], [pull(0, k) for k in range(1, half)], (vectors,))
    got, first = lax.optimization_barrier((got, first))
    got = exchange(total_of(got, far), "far")

    chained = [pull(1, k) for k in range(half // 2)]
    direct = [pull(0, k) for k in range(1, half)]
    second = lax.switch(plan_two[0], chained + direct, (vectors, first))
    got, second = lax.optimization_barrier((got, second))
    mine = got[:, :24].astype(jnp.float32).sum(0).astype(jnp.bfloat16)
    lines = got
    other = lax.ppermute(mine, "blk", [(i, i ^ 1) for i in range(blocks)])

    sums = pl.pallas_call(
        tiles_kernel,
        out_shape=jax.ShapeDtypeStruct((slices, count_piv * share, NOFF * rows), jnp.bfloat16),
        in_specs=[SMEM] + [VMEM] * 5,
        out_specs=VMEM,
        compiler_params=SMALL,
    )(swap, vectors, first, second, mine, other)
    got = lax.all_to_all(sums, "fld", 0, 0)

    return pl.pallas_call(
        finish_kernel,
        out_shape=jax.ShapeDtypeStruct((NOFF, count_piv, share, rows), jnp.bfloat16),
        in_specs=[SMEM, SMEM, SMEM, VMEM, VMEM, VMEM],
        out_specs=VMEM,
        compiler_params=SMALL,
    )(offsets, pivot_block, pivot_row, got, norms_row, lines)


def solution(mesh):
    return jax.shard_map(
        body,
        mesh=mesh,
        in_specs=(P("blk", "fld"), P("blk"), P(), P(), P()),
        out_specs=P(None, None, ("blk", "fld"), None),
        check_vma=False,
    )
```
